512 devices in a mesh: layer: 2 (over core), row: 16 (over x, z_hi), col: 16 (over z_lo, y).
Axes of the slice: x: 4, y: 8, z: 8 (z_hi: 4, z_lo: 2; z = z_hi * 2 + z_lo), core: 2. Of those that a mesh axis runs over, the one named last changes fastest.
Arguments:
- rhs_sub: float32 [2, 3, 1, 16, 256, 512], P('layer', None, None, 'row', 'col'), may hold values from -6 to 6
- rhs_top: float32 [1, 16, 256, 512], P(None, 'row', 'col'), may hold values from -6 to 6
- lower_inv_sub: float32 [2, 3, 1, 16, 256, 256], P('layer', None, None, 'row', 'col'), as said below
- lower_inv_top: float32 [1, 16, 256, 256], P(None, 'row', 'col'), as said below
- upper_inv_sub: float32 [2, 3, 1, 16, 256, 256], P('layer', None, None, 'row', 'col'), as said below
- upper_inv_top: float32 [1, 16, 256, 256], P(None, 'row', 'col'), as said below
- lower_sub: float32 [2, 3, 1, 16, 1, 16, 256, 256], P('layer', None, None, 'row', None, 'col'), may hold values from -0.09375 to 0.09375
- lower_top: float32 [2, 3, 1, 16, 1, 16, 256, 256], P('layer', None, None, 'row', None, 'col'), may hold values from -0.0546875 to 0.0546875
- upper_sub: float32 [2, 3, 1, 16, 1, 16, 256, 256], P('layer', None, None, 'row', None, 'col'), may hold values from -0.0625 to 0.0625
- upper_top: float32 [2, 3, 1, 16, 1, 16, 256, 256], P('layer', None, None, 'row', None, 'col'), may hold values from -0.09375 to 0.09375
- block_pattern: int32 [2, 4, 3, 1, 16, 1, 16], P('layer', None, None, None, 'row', None, 'col'), may hold values 0 or 1
Outputs:
- solution_sub: float32 [2, 3, 1, 16, 256, 512], P('layer', None, None, 'row', 'col')
- solution_top: float32 [1, 16, 256, 512], P(None, 'row', 'col')
The draws below stay inside these ranges and needn't reach their ends.
Inputs may be any that keep to these rules, and one draw needn't show every extreme that they name: `lower_inv_sub`: every 256 x 256 block is lower triangular with unit diagonal. `lower_inv_top`: every 256 x 256 block is lower triangular with unit diagonal. `upper_inv_sub`: every 256 x 256 block is upper triangular with unit diagonal. `upper_inv_top`: every 256 x 256 block is upper triangular with unit diagonal.
All inputs are finite; a program needn't handle non-finite values. No bound on the sum of `block_pattern` on one device may be relied on, other than what follows from the above.
Results may differ from the reference program's by a relative error of at most 0.00014.
Values sent between devices are 32-bit elements; how exact they have to be, the bound alone decides.
No kernel may reach another device: no remote copies, remote signals or barrier semaphores. Data moves between devices by JAX's collectives and lax.ppermute only.
A program may use at most 64 MiB of HBM per device.

```python
import math
import jax
import jax.numpy as jnp
from jax import lax

W = 256
NRHS = 512
SN_ROW = 1
LAYERS = 2
GRID = 16


def unit_triangle(noise, lower):
    shape = noise.shape
    down_index = lax.broadcasted_iota(jnp.int32, shape, len(shape) - 2)
    across_index = lax.broadcasted_iota(jnp.int32, shape, len(shape) - 1)
    strict = down_index > across_index if lower else down_index < across_index
    scaled = noise * (0.8 / math.sqrt(W))
    return jnp.where(down_index == across_index, 1.0, jnp.where(strict, scaled, 0.0)).astype(jnp.float32)


def draw_noise(key, shape):
    return jax.random.normal(key, shape, jnp.float32)


def draw_lower_inv_sub(key, part):
    return unit_triangle(draw_noise(key, (LAYERS, 3, SN_ROW, GRID, W, W)), True)


def draw_lower_inv_top(key, part):
    return unit_triangle(draw_noise(key, (SN_ROW, GRID, W, W)), True)


def draw_upper_inv_sub(key, part):
    return unit_triangle(draw_noise(key, (LAYERS, 3, SN_ROW, GRID, W, W)), False)


def draw_upper_inv_top(key, part):
    return unit_triangle(draw_noise(key, (SN_ROW, GRID, W, W)), False)


def plant(drawn, key, least, top_value):
    index_at = [jax.random.randint(jax.random.fold_in(key, axis), (), 0, length) for axis, length in enumerate(drawn.shape)]
    main_axis = drawn.shape.index(max(drawn.shape))
    beside = index_at[:main_axis] + [(index_at[main_axis] + 1) % drawn.shape[main_axis]] + index_at[main_axis + 1:]
    return drawn.at[tuple(index_at)].set(least).at[tuple(beside)].set(top_value)


def spiked(result, own_key, source, target, shards_of, factor):
    def block_of(axis_at):
        return (jnp.arange(result.shape[axis_at]) // (result.shape[axis_at] // shards_of)).reshape((-1,) + (1,) * (result.ndim - 1 - axis_at))

    first = jax.random.permutation(own_key, shards_of)[block_of(target)]
    second = (block_of(target) + shards_of // 2) % shards_of
    return jnp.where((block_of(source) == first) | (block_of(source) == second), factor * result, result)


def level_of(stream_key, dims, shards, least, top_value):
    def one(position, blocks):
        heights = jax.random.uniform(jax.random.fold_in(jax.random.fold_in(stream_key, 6), position), (blocks,), jnp.float32, least / len(shards), top_value / len(shards))
        return jnp.repeat(jnp.exp(heights), dims[position] // blocks).reshape((-1,) + (1,) * (len(dims) - position - 1))

    gain = one(*shards[0])
    for cut in shards[1:]:
        gain = gain * one(*cut)
    return gain


def scatter_about(own_key, dims, deviation, bound, pieces=(), held_as=jnp.bfloat16):
    entries = deviation * jax.random.normal(own_key, dims, jnp.float32)
    if pieces:
        entries = entries * level_of(own_key, dims, pieces, -0.22, 0.18)
    return jnp.clip(entries, -bound, bound).astype(held_as)


def heavy_noise(own_key, extent, width, most, split, heavy, dtype=jnp.bfloat16):
    drawn = width * jax.random.normal(own_key, extent, jnp.float32)
    if split:
        drawn = drawn * level_of(own_key, extent, split, -0.22, 0.18)
    return jnp.clip(spiked(drawn, jax.random.fold_in(own_key, 3), *heavy), -most, most).astype(dtype)


def setup_inputs(seed: int = 0) -> dict:
    key_list = jax.random.split(jax.random.key(seed), 12)
    return {
        "rhs_sub": scatter_about(key_list[0], (LAYERS, 3, SN_ROW, GRID, W, NRHS), 1.0, 6.0, ((0, 2), (3, 16), (4, 16)), jnp.float32),
        "rhs_top": scatter_about(key_list[1], (SN_ROW, GRID, W, NRHS), 1.0, 6.0, ((1, 16), (2, 16)), jnp.float32),
        "lower_inv_sub": draw_lower_inv_sub(jax.random.fold_in(key_list[11], 71), 0),
        "lower_inv_top": draw_lower_inv_top(jax.random.fold_in(key_list[11], 71), 0),
        "upper_inv_sub": draw_upper_inv_sub(jax.random.fold_in(key_list[11], 71), 0),
        "upper_inv_top": draw_upper_inv_top(jax.random.fold_in(key_list[11], 71), 0),
        "lower_sub": heavy_noise(key_list[6], (LAYERS, 3, SN_ROW, GRID, SN_ROW, GRID, W, W), (2 * W * SN_ROW * GRID) ** -0.5, 0.09375, ((0, 2), (3, 16), (5, 16)), (5, 6, 16, 2.0), jnp.float32),
        "lower_top": heavy_noise(key_list[7], (LAYERS, 3, SN_ROW, GRID, SN_ROW, GRID, W, W), (3 * LAYERS * W * SN_ROW * GRID) ** -0.5, 0.0546875, ((0, 2), (3, 16), (5, 16)), (5, 6, 16, 2.0), jnp.float32),
        "upper_sub": heavy_noise(key_list[8], (LAYERS, 3, SN_ROW, GRID, SN_ROW, GRID, W, W), (4 * W * SN_ROW * GRID) ** -0.5, 0.0625, ((0, 2), (3, 16), (5, 16)), (5, 6, 16, 2.0), jnp.float32),
        "upper_top": heavy_noise(key_list[9], (LAYERS, 3, SN_ROW, GRID, SN_ROW, GRID, W, W), (2 * W * SN_ROW * GRID) ** -0.5, 0.09375, ((0, 2), (3, 16), (5, 16)), (5, 6, 16, 2.0), jnp.float32),
        "block_pattern": plant((jax.random.randint(key_list[10], (LAYERS, 4, 3, SN_ROW, GRID, SN_ROW, GRID), 0, 4) < 3).astype(jnp.int32), jax.random.fold_in(key_list[10], 1), 0, 1),
    }


HIGHEST = lax.Precision.HIGHEST


def apply_inverse(inverse, block):
    return jnp.einsum('...ab,...bn->...an', inverse, block, precision=HIGHEST)


def couple(blocks, pattern, solution):
    masked = blocks * pattern[..., None, None].astype(jnp.float32)
    return jnp.einsum('tgsqab,sqbn->tgan', masked, solution, precision=HIGHEST)


def reference(rhs_sub, rhs_top, lower_inv_sub, lower_inv_top, upper_inv_sub, upper_inv_top, lower_sub, lower_top, upper_sub, upper_top, block_pattern):
    forward = []
    top_sum = jnp.zeros(rhs_top.shape, jnp.float32)
    for layer_index in range(LAYERS):
        pattern_layer = block_pattern[layer_index]
        fore_zero = apply_inverse(lower_inv_sub[layer_index, 0], rhs_sub[layer_index, 0])
        fore_one = apply_inverse(lower_inv_sub[layer_index, 1], rhs_sub[layer_index, 1] - couple(lower_sub[layer_index, 0], pattern_layer[0, 0], fore_zero))
        fore_two = apply_inverse(lower_inv_sub[layer_index, 2], rhs_sub[layer_index, 2] - couple(lower_sub[layer_index, 1], pattern_layer[0, 1], fore_zero) - couple(lower_sub[layer_index, 2], pattern_layer[0, 2], fore_one))
        top_sum = top_sum + couple(lower_top[layer_index, 0], pattern_layer[1, 0], fore_zero)
        top_sum = top_sum + couple(lower_top[layer_index, 1], pattern_layer[1, 1], fore_one)
        top_sum = top_sum + couple(lower_top[layer_index, 2], pattern_layer[1, 2], fore_two)
        forward.append((fore_zero, fore_one, fore_two))
    fore_top = apply_inverse(lower_inv_top, rhs_top - top_sum)
    final_top = apply_inverse(upper_inv_top, fore_top)
    finals = []
    for layer_index in range(LAYERS):
        pattern_layer = block_pattern[layer_index]
        fore_zero, fore_one, fore_two = forward[layer_index]
        final_two = apply_inverse(upper_inv_sub[layer_index, 2], fore_two - couple(upper_top[layer_index, 2], pattern_layer[3, 2], final_top))
        final_one = apply_inverse(upper_inv_sub[layer_index, 1], fore_one - couple(upper_sub[layer_index, 2], pattern_layer[2, 2], final_two) - couple(upper_top[layer_index, 1], pattern_layer[3, 1], final_top))
        final_zero = apply_inverse(upper_inv_sub[layer_index, 0], fore_zero - couple(upper_sub[layer_index, 0], pattern_layer[2, 0], final_one) - couple(upper_sub[layer_index, 1], pattern_layer[2, 1], final_two) - couple(upper_top[layer_index, 0], pattern_layer[3, 0], final_top))
        finals.append(jnp.stack([final_zero, final_one, final_two]))
    solution_sub = jnp.stack(finals)
    return solution_sub, final_top
```

```python
import jax
import jax.numpy as jnp
from jax import lax
from jax.sharding import Mesh, PartitionSpec as P

GRID = 16
SHARD = 16
XS = 4
HS = 4
NRHS = 512
COL = ("zl", "y")
ROW = ("x", "zh")
PLANE = ROW + COL
PARTS = 1
WIDE = NRHS // PARTS
STAGED = True


def dot(a, b):
    return jnp.dot(a, b, precision=lax.Precision.HIGH)


def gather(chunk, axes, size):
    spread = jnp.broadcast_to(chunk[None], (size,) + chunk.shape)
    return lax.all_to_all(spread, axes, 0, 0, tiled=True)


def gather_down(chunk):
    width = chunk.shape[1]
    if STAGED:
        part = gather(chunk, "zh", HS).reshape(HS * chunk.shape[0], width)
        return gather(part, "x", XS).reshape(GRID * chunk.shape[0], width)
    return gather(chunk, ROW, GRID).reshape(GRID * chunk.shape[0], width)


def turn(chunk):
    return lax.ppermute(chunk, PLANE, [(r * GRID + c, c * GRID + r) for r in range(GRID) for c in range(GRID)])


def reduce_row(partial):
    chunks = lax.all_to_all(partial.reshape(GRID, SHARD, partial.shape[1]), COL, 0, 0, tiled=True)
    return jnp.sum(chunks, axis=0)


def on_device(
    rhs_sub,
    rhs_top,
    lower_inv_sub,
    lower_inv_top,
    upper_inv_sub,
    upper_inv_top,
    lower_sub,
    lower_top,
    upper_sub,
    upper_top,
    block_pattern,
):
    row = lax.axis_index(ROW)
    col = lax.axis_index(COL)
    mine = (row == col).astype(jnp.float32)
    first_layer = (lax.axis_index("layer") == 0).astype(jnp.float32)

    def block(array, kind, pair):
        return array[0, pair, 0, 0, 0, 0] * block_pattern[0, kind, pair, 0, 0, 0, 0].astype(jnp.float32)

    lower_inv = jnp.concatenate([lower_inv_sub[0, :, 0, 0], lower_inv_top[:, 0]])
    upper_inv = jnp.concatenate([upper_inv_sub[0, :, 0, 0], upper_inv_top[:, 0]])
    row_at = lax.broadcasted_iota(jnp.int32, (4, SHARD, 256), 1) + col * SHARD
    col_at = lax.broadcasted_iota(jnp.int32, (4, SHARD, 256), 2)
    packed = gather(jnp.where(col_at < row_at, lower_inv, upper_inv), COL, GRID)
    packed = packed.reshape(GRID, 4, SHARD, 256)
    down = lax.broadcasted_iota(jnp.int32, (256, 256), 0)
    across = lax.broadcasted_iota(jnp.int32, (256, 256), 1)
    unit = jnp.where(down == across, 1.0, 0.0)
    whole = [packed[:, k].reshape(256, 256) for k in range(4)]
    lower = [jnp.where(across < down, m, unit) for m in whole]
    upper = [jnp.where(across >= down, m, 0.0) for m in whole]
    top = dot(upper[3], lower[3])

    def columns(matrix):
        return lax.dynamic_slice(matrix, (0, col * SHARD), (256, SHARD))

    start = jnp.concatenate([lower_inv_sub[0, 0, 0, 0], rhs_sub[0, 0, 0, 0]], axis=1)
    start = gather_down(turn(start))
    inverse0 = start[:, :256]

    own1 = columns(lower[1])
    own2 = columns(lower[2])
    own3 = columns(top) * first_layer
    low10 = dot(lower[1], block(lower_sub, 0, 0))
    low20 = dot(lower[2], block(lower_sub, 0, 1))
    low21 = dot(lower[2], block(lower_sub, 0, 2))
    top0 = dot(top, block(lower_top, 1, 0))
    top1 = dot(top, block(lower_top, 1, 1))
    top2 = dot(top, block(lower_top, 1, 2))
    up23 = dot(upper[2], block(upper_top, 3, 2))
    up13 = dot(upper[1], block(upper_top, 3, 1))
    up03 = dot(upper[0], block(upper_top, 3, 0))
    up12 = dot(upper[1], block(upper_sub, 2, 2))
    up02 = dot(upper[0], block(upper_sub, 2, 1))
    up01 = dot(upper[0], block(upper_sub, 2, 0))
    diag2 = upper[2] * mine
    diag1 = upper[1] * mine
    diag0 = upper[0] * mine

    parts = range(PARTS)

    def share(array):
        return [array[:, p * WIDE:(p + 1) * WIDE] for p in parts]

    def each(function, *lists):
        return [function(*items) for items in zip(*lists)]

    y0 = each(lambda v: dot(inverse0, v), share(start[:, 256:]))

    y1 = each(lambda r, a: reduce_row(dot(own1, r) - dot(low10, a)), share(rhs_sub[0, 1, 0, 0]), y0)
    share2 = each(lambda r, a: dot(own2, r) - dot(low20, a), share(rhs_sub[0, 2, 0, 0]), y0)
    share3 = each(lambda r, a: dot(own3, r) - dot(top0, a), share(rhs_top[0, 0]), y0)
    y1 = each(gather_down, each(turn, y1))
    y2 = each(lambda s, a: reduce_row(s - dot(low21, a)), share2, y1)
    share3 = each(lambda s, a: s - dot(top1, a), share3, y1)
    y2 = each(gather_down, each(turn, y2))

    def swap(v):
        return lax.ppermute(v, "layer", [(0, 1), (1, 0)])

    def across_layers(chunk):
        return chunk + swap(chunk)

    final3 = each(lambda s, a: across_layers(reduce_row(s - dot(top2, a))), share3, y2)
    share2 = each(lambda a: dot(diag2, a), y2)
    share1 = each(lambda a: dot(diag1, a), y1)
    share0 = each(lambda a: dot(diag0, a), y0)
    x3 = each(gather_down, each(turn, final3))

    final2 = each(lambda s, a: reduce_row(s - dot(up23, a)), share2, x3)
    share1 = each(lambda s, a: s - dot(up13, a), share1, x3)
    share0 = each(lambda s, a: s - dot(up03, a), share0, x3)
    x2 = each(gather_down, each(turn, final2))
    final1 = each(lambda s, a: reduce_row(s - dot(up12, a)), share1, x2)
    share0 = each(lambda s, a: s - dot(up02, a), share0, x2)
    x1 = each(gather_down, each(turn, final1))
    final0 = each(lambda s, a: reduce_row(s - dot(up01, a)), share0, x1)

    solution_sub = jnp.stack([jnp.concatenate(v, axis=1) for v in (final0, final1, final2)])
    solution_top = jnp.concatenate(final3, axis=1)
    return solution_sub[None, :, None, None], solution_top[None, None]


def solution(mesh):
    fine = Mesh(mesh.devices.reshape(2, 4, 4, 2, 8), ("layer",) + PLANE)
    vector = P("layer", None, None, ROW, COL, None)
    vector_top = P(None, ROW, COL, None)
    blocks = P("layer", None, None, ROW, None, COL, None, None)
    pattern = P("layer", None, None, None, ROW, None, COL)
    placed = (vector, vector_top, vector, vector_top, vector, vector_top, blocks, blocks, blocks, blocks, pattern)
    return jax.shard_map(on_device, mesh=fine, in_specs=placed, out_specs=(vector, vector_top), check_vma=False)
```

```python
import jax
import jax.numpy as jnp
from jax import lax
from jax.sharding import Mesh, PartitionSpec as P


W = 256
HALF = 256
GRID = 16
SHARD = 16
YS = 8
CHUNK = 2 * SHARD
COL = ("zl", "y")
ROW = ("x", "zh")
PLANE = ROW + COL
SWAP = [(0, 1), (1, 0)]
NEAR = (
    (6, 7, 3, 4, 0, 1, 5, 2),
    (3, 7, 4, 0, 5, 1, 2, 6),
    (1, 0, 4, 5, 7, 6, 2, 3),
    (0, 2, 4, 5, 1, 6, 7, 3),
    (4, 0, 5, 6, 2, 1, 3, 7),
    (1, 5, 4, 6, 2, 3, 7, 0),
    (5, 2, 6, 7, 3, 1, 0, 4),
    (2, 6, 3, 7, 4, 0, 5, 1),
)
PLAIN = tuple(tuple(range(YS)) for _ in range(YS))


def dot(a, b):
    return jnp.dot(a, b, precision=lax.Precision.HIGH)


def turn(chunk, table):
    pairs = []
    for r in range(GRID):
        for zl in range(2):
            for y in range(YS):
                target = (r // YS) * YS + table[r % YS][y]
                pairs.append((r * GRID + zl * YS + y, target * GRID + zl * YS + r % YS))
    return lax.ppermute(chunk, PLANE, pairs)


def gather(chunk, axes, size):
    return lax.all_to_all(jnp.broadcast_to(chunk[None], (size,) + chunk.shape), axes, 0, 0, tiled=True)


def gather_down(chunk):
    return gather(chunk, ROW, GRID).reshape(GRID * chunk.shape[0], chunk.shape[1])


def reduce_row(partial):
    return jnp.sum(lax.all_to_all(partial.reshape(YS, CHUNK, partial.shape[1]), "y", 0, 0, tiled=True), axis=0)


def reduce_layers(partial):
    halves = partial.reshape(W, 2, HALF // 2).transpose(1, 0, 2)
    return jnp.sum(lax.all_to_all(halves, "layer", 0, 0, tiled=True), axis=0)


def gather_layers(part):
    return gather(part, "layer", 2).transpose(1, 0, 2).reshape(part.shape[0], HALF)


def on_device(
    rhs_sub,
    rhs_top,
    lower_inv_sub,
    lower_inv_top,
    upper_inv_sub,
    upper_inv_top,
    lower_sub,
    lower_top,
    upper_sub,
    upper_top,
    block_pattern,
):
    layer = lax.axis_index("layer")
    row = lax.axis_index(ROW)
    col = lax.axis_index(COL)
    y_at = lax.axis_index("y")
    even = lax.axis_index("zl") == 0

    def ordered(own, other, axis, first=even):
        return jnp.where(first, jnp.concatenate([own, other], axis), jnp.concatenate([other, own], axis))

    lower_inv = jnp.concatenate([lower_inv_sub[0, :, 0, 0], lower_inv_top[:, 0]])
    upper_inv = jnp.concatenate([upper_inv_sub[0, :, 0, 0], upper_inv_top[:, 0]])
    row_at = lax.broadcasted_iota(jnp.int32, (4, SHARD, W), 1) + col * SHARD
    col_at = lax.broadcasted_iota(jnp.int32, (4, SHARD, W), 2)
    packed = gather(jnp.where(col_at < row_at, lower_inv, upper_inv), COL, GRID)

    rhs = jnp.concatenate([rhs_sub[0, :, 0, 0], rhs_top[:, 0]])
    keep = jnp.where(even, rhs[:, :, :HALF], rhs[:, :, HALF:])
    send = jnp.where(even, rhs[:, :, HALF:], rhs[:, :, :HALF])
    got = lax.ppermute(jnp.concatenate([send, lower_inv_sub[0, :1, 0, 0]]), "zl", SWAP)
    rhs = ordered(keep, got[:4], 1)
    start = jnp.concatenate([ordered(lower_inv_sub[0, 0, 0, 0], got[4], 0), rhs[0]], axis=1)
    start = turn(start, PLAIN)
    start = gather_down(start)

    def masked(array, kind):
        return array[0, :, 0, 0, 0, 0] * block_pattern[0, kind, :, 0, 0, 0, 0].astype(jnp.float32)[:, None, None]

    def both(own):
        other = lax.ppermute(own, "zl", SWAP)
        return [ordered(own[pair], other[pair], 1) for pair in range(own.shape[0])]

    low_own = masked(lower_sub, 0)
    low_sub = both(low_own[:1]) + both(low_own[1:])
    low_top = both(masked(lower_top, 1))
    up_top = both(masked(upper_top, 3))
    up_sub = both(masked(upper_sub, 2))

    packed = packed.reshape(GRID, 4, SHARD, W)
    natural = lax.broadcasted_iota(jnp.int32, (W, W), 0)
    across = lax.broadcasted_iota(jnp.int32, (W, W), 1)
    table = jnp.array(NEAR, jnp.int32)
    mine = lax.dynamic_index_in_dim(table, row % YS, 0, keepdims=False)
    slot = natural // CHUNK
    moved = natural % CHUNK
    for y in range(YS):
        moved = moved + jnp.where(slot == y, mine[y] * CHUNK, 0)
    pick = (across == moved).astype(jnp.float32)
    whole = [packed[:, k].reshape(W, W) for k in range(4)]
    near = [None] + [jnp.dot(pick, whole[k], precision=lax.Precision.HIGHEST) for k in (1, 2, 3)]

    def lower_of(matrix, down):
        return jnp.where(across < down, matrix, jnp.where(across == down, 1.0, 0.0))

    def upper_of(matrix, down):
        return jnp.where(across >= down, matrix, 0.0)

    lower1 = lower_of(near[1], moved)
    lower2 = lower_of(near[2], moved)
    top = dot(upper_of(near[3], moved), lower_of(whole[3], natural))
    upper2 = upper_of(near[2], moved)
    upper1 = upper_of(near[1], moved)
    upper0 = upper_of(whole[0], natural)
    upper0 = upper0.reshape(2, YS, SHARD, W).transpose(1, 0, 2, 3).reshape(W, W)

    def columns(matrix):
        left = lax.dynamic_slice(matrix, (0, y_at * SHARD), (W, SHARD))
        right = lax.dynamic_slice(matrix, (0, W // 2 + y_at * SHARD), (W, SHARD))
        return jnp.concatenate([left, right], axis=1)

    low10 = dot(lower1, low_sub[0])
    share1 = dot(columns(lower1), rhs[1])
    share2 = dot(columns(lower2), rhs[2])
    share3 = dot(columns(top), rhs[3]) * (layer == 0).astype(jnp.float32)

    own_column = (row % YS == y_at).astype(jnp.float32)
    diag2 = upper2 * own_column
    diag1 = upper1 * own_column
    diag0 = upper0 * own_column

    def own(pair):
        return jnp.where(row < YS, pair[:W], pair[W:])

    start = start.reshape(2, YS, 2, SHARD, W + HALF).transpose(0, 2, 1, 3, 4).reshape(2, W, W + HALF)
    y0 = jnp.concatenate([dot(start[s, :, :W], start[s, :, W:]) for s in range(2)])

    y1 = reduce_row(share1 - dot(low10, y0))
    y1 = turn(y1, NEAR)
    low20 = dot(lower2, low_sub[1])
    low21 = dot(lower2, low_sub[2])
    share2 = share2 - dot(low20, y0)
    y1 = gather_down(y1)

    y2 = reduce_row(share2 - dot(low21, y1))
    y2 = turn(y2, NEAR)
    share3 = share3 - dot(dot(top, low_top[0]), y0)
    share3 = share3 - dot(dot(top, low_top[1]), y1)
    top2 = dot(top, low_top[2])
    y2 = gather_down(y2)

    x3 = reduce_layers(share3 - dot(top2, y2))
    final3 = reduce_row(x3)
    x3 = turn(final3, NEAR)
    back0 = dot(diag0, own(y0))
    back1 = dot(diag1, own(y1))
    back2 = dot(diag2, own(y2))
    up23 = dot(upper2, up_top[2])
    x3 = gather_down(x3)
    x3 = gather_layers(x3)
    final3 = ordered(final3, lax.ppermute(final3, "layer", SWAP), 1, layer == 0)

    final2 = reduce_row(back2 - dot(up23, x3))
    x2 = turn(final2, NEAR)
    up12 = dot(upper1, up_sub[2])
    back1 = back1 - dot(dot(upper1, up_top[1]), x3)
    back0 = back0 - dot(dot(upper0, up_top[0]), x3)
    x2 = gather_down(x2)

    final1 = reduce_row(back1 - dot(up12, x2))
    x1 = turn(final1, NEAR)
    up01 = dot(upper0, up_sub[0])
    back0 = back0 - dot(dot(upper0, up_sub[1]), x2)
    x1 = gather_down(x1)

    final0 = reduce_row(back0 - dot(up01, x1))

    solved = jnp.stack([final1, final2, final3])
    upper_rows, lower_rows = solved[:, :SHARD], solved[:, SHARD:]
    straight, crossed = [], []
    for r in range(GRID):
        for zl in range(2):
            for y in range(YS):
                target = r * GRID + 2 * NEAR[r % YS][y]
                straight.append((r * GRID + zl * YS + y, target + zl))
                crossed.append((r * GRID + zl * YS + y, target + 1 - zl))
    first = lax.ppermute(jnp.where(even, upper_rows, lower_rows), PLANE, straight)
    second = lax.ppermute(jnp.where(even, lower_rows, upper_rows), PLANE, crossed)
    solved = ordered(first, second, 2, y_at % 2 == 0)
    kept = jnp.where(even, final0[:SHARD], final0[SHARD:])
    sent = jnp.where(even, final0[SHARD:], final0[:SHARD])
    final0 = ordered(kept, lax.ppermute(sent, "zl", SWAP), 1)
    solution_sub = jnp.concatenate([final0[None], solved[:2]])
    return solution_sub[None, :, None, None], solved[2:, None]


def solution(mesh):
    fine = Mesh(mesh.devices.reshape(2, 4, 4, 2, 8), ("layer",) + PLANE)
    vector = P("layer", None, None, ROW, COL, None)
    vector_top = P(None, ROW, COL, None)
    blocks = P("layer", None, None, ROW, None, COL, None, None)
    pattern = P("layer", None, None, None, ROW, None, COL)
    placed = (vector, vector_top, vector, vector_top, vector, vector_top, blocks, blocks, blocks, blocks, pattern)
    return jax.shard_map(on_device, mesh=fine, in_specs=placed, out_specs=(vector, vector_top), check_vma=False)
```

```python
import jax
import jax.numpy as jnp
from jax import lax
from jax.sharding import Mesh, PartitionSpec as P


W = 256
HALF = 256
GRID = 16
SHARD = 16
YS = 8
CHUNK = 2 * SHARD
COL = ("zl", "y")
ROW = ("x", "zh")
PLANE = ROW + COL
SWAP = [(0, 1), (1, 0)]
NEAR = (
    (6, 7, 3, 4, 0, 1, 5, 2),
    (3, 7, 4, 0, 5, 1, 2, 6),
    (1, 0, 4, 5, 7, 6, 2, 3),
    (0, 2, 4, 5, 1, 6, 7, 3),
    (4, 0, 5, 6, 2, 1, 3, 7),
    (1, 5, 4, 6, 2, 3, 7, 0),
    (5, 2, 6, 7, 3, 1, 0, 4),
    (2, 6, 3, 7, 4, 0, 5, 1),
)
PLAIN = tuple(tuple(range(YS)) for _ in range(YS))


def dot(a, b):
    return jnp.dot(a, b, precision=lax.Precision.HIGH)


def turn(chunk, table):
    pairs = []
    for r in range(GRID):
        for zl in range(2):
            for y in range(YS):
                target = (r // YS) * YS + table[r % YS][y]
                pairs.append((r * GRID + zl * YS + y, target * GRID + zl * YS + r % YS))
    return lax.ppermute(chunk, PLANE, pairs)


def gather(chunk, axes, size):
    return lax.all_to_all(jnp.broadcast_to(chunk[None], (size,) + chunk.shape), axes, 0, 0, tiled=True)


def gather_down(chunk):
    return gather(chunk, ROW, GRID).reshape(GRID * chunk.shape[0], chunk.shape[1])


def reduce_row(partial):
    return jnp.sum(lax.all_to_all(partial.reshape(YS, CHUNK, partial.shape[1]), "y", 0, 0, tiled=True), axis=0)


def reduce_layers(partial):
    halves = partial.reshape(W, 2, HALF // 2).transpose(1, 0, 2)
    return jnp.sum(lax.all_to_all(halves, "layer", 0, 0, tiled=True), axis=0)


def gather_layers(part):
    return gather(part, "layer", 2).transpose(1, 0, 2).reshape(part.shape[0], HALF)


def on_device(
    rhs_sub,
    rhs_top,
    lower_inv_sub,
    lower_inv_top,
    upper_inv_sub,
    upper_inv_top,
    lower_sub,
    lower_top,
    upper_sub,
    upper_top,
    block_pattern,
):
    layer = lax.axis_index("layer")
    row = lax.axis_index(ROW)
    col = lax.axis_index(COL)
    y_at = lax.axis_index("y")
    even = lax.axis_index("zl") == 0

    def ordered(own, other, axis, first=even):
        return jnp.where(first, jnp.concatenate([own, other], axis), jnp.concatenate([other, own], axis))

    lower_inv = jnp.concatenate([lower_inv_sub[0, :, 0, 0], lower_inv_top[:, 0]])
    upper_inv = jnp.concatenate([upper_inv_sub[0, :, 0, 0], upper_inv_top[:, 0]])
    row_at = lax.broadcasted_iota(jnp.int32, (4, SHARD, W), 1) + col * SHARD
    col_at = lax.broadcasted_iota(jnp.int32, (4, SHARD, W), 2)
    packed = gather(jnp.where(col_at < row_at, lower_inv, upper_inv), "y", YS)
    packed = packed.transpose(1, 0, 2, 3).reshape(4, W // 2, W)
    packed1 = lax.ppermute(packed[1], "zl", SWAP)
    packed2 = lax.ppermute(jnp.concatenate([packed[:1], packed[2:]]), "zl", SWAP)
    whole1 = ordered(packed[1], packed1, 0)

    rhs = jnp.concatenate([rhs_sub[0, :, 0, 0], rhs_top[:, 0]])
    keep = jnp.where(even, rhs[:, :, :HALF], rhs[:, :, HALF:])
    send = jnp.where(even, rhs[:, :, HALF:], rhs[:, :, :HALF])
    got = lax.ppermute(jnp.concatenate([send, lower_inv_sub[0, :1, 0, 0]]), "zl", SWAP)
    rhs = ordered(keep, got[:4], 1)
    start = jnp.concatenate([ordered(lower_inv_sub[0, 0, 0, 0], got[4], 0), rhs[0]], axis=1)
    start = turn(start, PLAIN)
    start = gather_down(start)

    def masked(array, kind):
        return array[0, :, 0, 0, 0, 0] * block_pattern[0, kind, :, 0, 0, 0, 0].astype(jnp.float32)[:, None, None]

    def both(own):
        other = lax.ppermute(own, "zl", SWAP)
        return [ordered(own[pair], other[pair], 1) for pair in range(own.shape[0])]

    low_own = masked(lower_sub, 0)
    low_sub = both(low_own[:1]) + both(low_own[1:])
    low_top = both(masked(lower_top, 1))
    up_top = both(masked(upper_top, 3))
    up_sub = both(masked(upper_sub, 2))

    natural = lax.broadcasted_iota(jnp.int32, (W, W), 0)
    across = lax.broadcasted_iota(jnp.int32, (W, W), 1)
    table = jnp.array(NEAR, jnp.int32)
    mine = lax.dynamic_index_in_dim(table, row % YS, 0, keepdims=False)
    slot = natural // CHUNK
    moved = natural % CHUNK
    for y in range(YS):
        moved = moved + jnp.where(slot == y, mine[y] * CHUNK, 0)
    pick = (across == moved).astype(jnp.float32)
    near1 = jnp.dot(pick, whole1, precision=lax.Precision.HIGHEST)

    def lower_of(matrix, down):
        return jnp.where(across < down, matrix, jnp.where(across == down, 1.0, 0.0))

    def upper_of(matrix, down):
        return jnp.where(across >= down, matrix, 0.0)

    lower1 = lower_of(near1, moved)
    upper1 = upper_of(near1, moved)

    def columns(matrix):
        left = lax.dynamic_slice(matrix, (0, y_at * SHARD), (W, SHARD))
        right = lax.dynamic_slice(matrix, (0, W // 2 + y_at * SHARD), (W, SHARD))
        return jnp.concatenate([left, right], axis=1)

    low10 = dot(lower1, low_sub[0])
    share1 = dot(columns(lower1), rhs[1])

    def own(pair):
        return jnp.where(row < YS, pair[:W], pair[W:])

    start = start.reshape(2, YS, 2, SHARD, W + HALF).transpose(0, 2, 1, 3, 4).reshape(2, W, W + HALF)
    y0 = jnp.concatenate([dot(start[s, :, :W], start[s, :, W:]) for s in range(2)])

    y1 = reduce_row(share1 - dot(low10, y0))
    packed2 = lax.optimization_barrier((packed2, y1))[0]
    y1 = turn(y1, NEAR)
    whole0, whole2, whole3 = [ordered(packed[k], packed2[j], 0) for j, k in enumerate((0, 2, 3))]
    near2 = jnp.dot(pick, whole2, precision=lax.Precision.HIGHEST)
    near3 = jnp.dot(pick, whole3, precision=lax.Precision.HIGHEST)
    lower2 = lower_of(near2, moved)
    top = dot(upper_of(near3, moved), lower_of(whole3, natural))
    upper2 = upper_of(near2, moved)
    upper0 = upper_of(whole0, natural)
    upper0 = upper0.reshape(2, YS, SHARD, W).transpose(1, 0, 2, 3).reshape(W, W)
    share2 = dot(columns(lower2), rhs[2])
    share3 = dot(columns(top), rhs[3]) * (layer == 0).astype(jnp.float32)
    own_column = (row % YS == y_at).astype(jnp.float32)
    diag2 = upper2 * own_column
    diag1 = upper1 * own_column
    diag0 = upper0 * own_column
    low20 = dot(lower2, low_sub[1])
    low21 = dot(lower2, low_sub[2])
    share2 = share2 - dot(low20, y0)
    y1 = gather_down(y1)

    y2 = reduce_row(share2 - dot(low21, y1))
    y2 = turn(y2, NEAR)
    share3 = share3 - dot(dot(top, low_top[0]), y0)
    share3 = share3 - dot(dot(top, low_top[1]), y1)
    top2 = dot(top, low_top[2])
    y2 = gather_down(y2)

    x3 = reduce_layers(share3 - dot(top2, y2))
    final3 = reduce_row(x3)
    x3 = turn(final3, NEAR)
    back0 = dot(diag0, own(y0))
    back1 = dot(diag1, own(y1))
    back2 = dot(diag2, own(y2))
    up23 = dot(upper2, up_top[2])
    x3 = gather_down(x3)
    x3 = gather_layers(x3)
    final3 = ordered(final3, lax.ppermute(final3, "layer", SWAP), 1, layer == 0)

    final2 = reduce_row(back2 - dot(up23, x3))
    x2 = turn(final2, NEAR)
    up12 = dot(upper1, up_sub[2])
    back1 = back1 - dot(dot(upper1, up_top[1]), x3)
    back0 = back0 - dot(dot(upper0, up_top[0]), x3)
    x2 = gather_down(x2)

    final1 = reduce_row(back1 - dot(up12, x2))
    x1 = turn(final1, NEAR)
    up01 = dot(upper0, up_sub[0])
    back0 = back0 - dot(dot(upper0, up_sub[1]), x2)
    x1 = gather_down(x1)

    final0 = reduce_row(back0 - dot(up01, x1))

    solved = jnp.stack([final1, final2, final3])
    upper_rows, lower_rows = solved[:, :SHARD], solved[:, SHARD:]
    straight, crossed = [], []
    for r in range(GRID):
        for zl in range(2):
            for y in range(YS):
                target = r * GRID + 2 * NEAR[r % YS][y]
                straight.append((r * GRID + zl * YS + y, target + zl))
                crossed.append((r * GRID + zl * YS + y, target + 1 - zl))
    first = lax.ppermute(jnp.where(even, upper_rows, lower_rows), PLANE, straight)
    second = lax.ppermute(jnp.where(even, lower_rows, upper_rows), PLANE, crossed)
    solved = ordered(first, second, 2, y_at % 2 == 0)
    kept = jnp.where(even, final0[:SHARD], final0[SHARD:])
    sent = jnp.where(even, final0[SHARD:], final0[:SHARD])
    final0 = ordered(kept, lax.ppermute(sent, "zl", SWAP), 1)
    solution_sub = jnp.concatenate([final0[None], solved[:2]])
    return solution_sub[None, :, None, None], solved[2:, None]


def solution(mesh):
    fine = Mesh(mesh.devices.reshape(2, 4, 4, 2, 8), ("layer",) + PLANE)
    vector = P("layer", None, None, ROW, COL, None)
    vector_top = P(None, ROW, COL, None)
    blocks = P("layer", None, None, ROW, None, COL, None, None)
    pattern = P("layer", None, None, None, ROW, None, COL)
    placed = (vector, vector_top, vector, vector_top, vector, vector_top, blocks, blocks, blocks, blocks, pattern)
    return jax.shard_map(on_device, mesh=fine, in_specs=placed, out_specs=(vector, vector_top), check_vma=False)
```
